32 devices in a mesh: dp: 4 (over x, core), ctx: 2 (over y), tensor: 4 (over z).
Axes of the slice: x: 2, y: 2, z: 4, core: 2. Of those that a mesh axis runs over, the one named last changes fastest.
Arguments:
- block_input: bfloat16 [8, 256, 1024], P('dp', 'ctx'), may hold values from -6 to 6
- out_cotangent: bfloat16 [8, 256, 1024], P('dp', 'ctx'), may hold values from -6 to 6
- gain_attn: bfloat16 [1024], P('dp'), may hold values from 0.5 to 1.5
- shift_attn: bfloat16 [1024], P('dp'), may hold values from -3 to 3
- qkv_weight: bfloat16 [3, 1024, 1024], P(None, 'dp', 'tensor'), may hold values from -0.1875 to 0.1875
- qv_bias: bfloat16 [2, 16, 64], P(None, 'tensor', 'dp'), may hold values from -3 to 3
- dense_weight: bfloat16 [1024, 1024], P('tensor', 'dp'), may hold values from -0.75 to 0.75
- dense_bias: bfloat16 [1024], P('dp'), may hold values from -3 to 3
- gain_mlp: bfloat16 [1024], P('dp'), may hold values from 0.5 to 1.5
- shift_mlp: bfloat16 [1024], P('dp'), may hold values from -3 to 3
- up_weight: bfloat16 [1024, 4096], P('dp', 'tensor'), may hold values from -0.1875 to 0.1875
- up_bias: bfloat16 [64, 64], P('tensor', 'dp'), may hold values from -3 to 3
- down_weight: bfloat16 [4096, 1024], P('tensor', 'dp'), may hold values from -0.09375 to 0.09375
- down_bias: bfloat16 [1024], P('dp'), may hold values from -3 to 3
Outputs:
- block_output: bfloat16 [8, 256, 1024], P('dp', 'ctx')
- grad_input: float32 [8, 256, 1024], P('dp', 'ctx')
- grad_gain_attn: float32 [1024], P('dp')
- grad_shift_attn: float32 [1024], P('dp')
- grad_qkv_weight: float32 [3, 1024, 1024], P(None, 'dp', 'tensor')
- grad_qv_bias: float32 [2, 16, 64], P(None, 'tensor', 'dp')
- grad_dense_weight: float32 [1024, 1024], P('tensor', 'dp')
- grad_dense_bias: float32 [1024], P('dp')
- grad_gain_mlp: float32 [1024], P('dp')
- grad_shift_mlp: float32 [1024], P('dp')
- grad_up_weight: float32 [1024, 4096], P('dp', 'tensor')
- grad_up_bias: float32 [64, 64], P('tensor', 'dp')
- grad_down_weight: float32 [4096, 1024], P('tensor', 'dp')
- grad_down_bias: float32 [1024], P('dp')
The draws below stay inside these ranges and needn't reach their ends.
All inputs are finite; a program needn't handle non-finite values.
Results may differ from the reference program's by a relative error of at most 0.023.
Values may be sent and summed in bfloat16 or wider, within the bound.
No kernel may reach another device: no remote copies, remote signals or barrier semaphores. Data moves between devices by JAX's collectives and lax.ppermute only.
A program may use at most 128 MiB of HBM per device.

```python
import math
import jax
import jax.numpy as jnp
from jax import lax

D = 1024
H = 16
HD = 64
FF = 4096
SEQS = 8
LEN = 256


def block_levels(key, dims, shards, low, largest):
    def one(axis_at, parts):
        draws = jax.random.uniform(jax.random.fold_in(jax.random.fold_in(key, 6), axis_at), (parts,), jnp.float32, low / len(shards), largest / len(shards))
        return jnp.repeat(jnp.exp(draws), dims[axis_at] // parts).reshape((-1,) + (1,) * (len(dims) - axis_at - 1))

    factor_of = one(*shards[0])
    for cut in shards[1:]:
        factor_of = factor_of * one(*cut)
    return factor_of


def normal_values(rng, dims, spread, bound, pieces=(), held_as=jnp.bfloat16):
    entries = jax.random.normal(rng, dims, jnp.float32) * spread
    if len(pieces) > 0:
        entries = block_levels(rng, dims, pieces, -0.22, 0.18) * entries
    return jnp.clip(entries, min=-bound, max=bound).astype(held_as)


def setup_inputs(seed: int = 0) -> dict:
    splits = jax.random.split(jax.random.key(seed), 15)
    block_input = normal_values(splits[0], (SEQS, LEN, D), 1.0, 6.0, ((0, 4), (1, 2)))
    out_cotangent = normal_values(splits[1], (SEQS, LEN, D), 1.0, 6.0, ((0, 4), (1, 2)))
    gain_attn = jnp.clip(1.0 + 0.1 * jax.random.normal(splits[2], (D,), jnp.float32), 0.5, 1.5).astype(jnp.bfloat16)
    shift_attn = normal_values(splits[3], (D,), 0.5, 3.0, ((0, 4),))
    qkv_weight = normal_values(splits[4], (3, D, D), D ** -0.5, 0.1875, ((1, 4), (2, 4)))
    qv_bias = normal_values(splits[5], (2, H, HD), 0.5, 3.0, ((1, 4), (2, 4)))
    dense_weight = normal_values(splits[6], (D, D), HD ** -0.5, 0.75, ((0, 4), (1, 4)))
    dense_bias = normal_values(splits[7], (D,), 0.5, 3.0, ((0, 4),))
    gain_mlp = jnp.clip(1.0 + 0.1 * jax.random.normal(splits[8], (D,), jnp.float32), 0.5, 1.5).astype(jnp.bfloat16)
    shift_mlp = normal_values(splits[9], (D,), 0.5, 3.0, ((0, 4),))
    up_weight = normal_values(splits[10], (D, FF), D ** -0.5, 0.1875, ((0, 4), (1, 4)))
    up_bias = normal_values(splits[11], (FF // HD, HD), 0.5, 3.0, ((0, 4), (1, 4)))
    down_weight = normal_values(splits[12], (FF, D), FF ** -0.5, 0.09375, ((0, 4), (1, 4)))
    down_bias = normal_values(splits[13], (D,), 0.5, 3.0, ((0, 4),))
    return dict(block_input=block_input, out_cotangent=out_cotangent, gain_attn=gain_attn, shift_attn=shift_attn, qkv_weight=qkv_weight, qv_bias=qv_bias, dense_weight=dense_weight, dense_bias=dense_bias, gain_mlp=gain_mlp, shift_mlp=shift_mlp, up_weight=up_weight, up_bias=up_bias, down_weight=down_weight, down_bias=down_bias)


eps = 1e-05
negative_big = -1e+30

def norm_forward(rows, gain, shift):
    center = rows - lax.optimization_barrier(jnp.mean(rows, axis=-1, keepdims=True))
    scale = lax.rsqrt(lax.optimization_barrier(jnp.mean(center * center, axis=-1, keepdims=True)) + eps)
    return center * scale * gain + shift

def gelu_tanh(values):
    return jax.nn.gelu(values, approximate=True)

def reference(block_input, out_cotangent, gain_attn, shift_attn, qkv_weight, qv_bias, dense_weight, dense_bias, gain_mlp, shift_mlp, up_weight, up_bias, down_weight, down_bias):
    gain_one = gain_attn.astype(jnp.float32)
    shift_one = shift_attn.astype(jnp.float32)
    gain_two = gain_mlp.astype(jnp.float32)
    shift_two = shift_mlp.astype(jnp.float32)
    bias_query = qv_bias[0].reshape(D).astype(jnp.float32)
    bias_value = qv_bias[1].reshape(D).astype(jnp.float32)
    bias_dense = dense_bias.astype(jnp.float32)
    bias_up = up_bias.reshape(FF).astype(jnp.float32)
    bias_down = down_bias.astype(jnp.float32)
    slopes = 2.0 ** (-8.0 * (jnp.arange(H, dtype=jnp.float32) + 1.0) / H)
    block = math.gcd(LEN, 512)
    blocks = LEN // block
    positions = jnp.arange(LEN, dtype=jnp.int32)
    scale = HD ** (-0.5)

    def scores_of(queries_part, keys, start):
        query_pos = start + jnp.arange(block, dtype=jnp.int32)
        raw = jnp.einsum('qhd,khd->hqk', queries_part.astype(jnp.float32), keys.astype(jnp.float32)) * scale
        distance = (query_pos[:, None] - positions[None, :]).astype(jnp.float32)
        raw = raw - slopes[:, None, None] * distance[None]
        allowed = (positions[None, :] <= query_pos[:, None])[None]
        return (jnp.where(allowed, raw, negative_big), allowed)

    def one_sequence(grads, pair):
        inputs, cotangent = pair
        rows_in = inputs.astype(jnp.float32)
        normed_low = norm_forward(rows_in, gain_one, shift_one).astype(jnp.bfloat16)
        queries = (jnp.dot(normed_low, qkv_weight[0], preferred_element_type=jnp.float32) + bias_query).astype(jnp.bfloat16).reshape(LEN, H, HD)
        keys = jnp.dot(normed_low, qkv_weight[1], preferred_element_type=jnp.float32).astype(jnp.bfloat16).reshape(LEN, H, HD)
        values = (jnp.dot(normed_low, qkv_weight[2], preferred_element_type=jnp.float32) + bias_value).astype(jnp.bfloat16).reshape(LEN, H, HD)

        def forward_block(index):
            start = index * block
            queries_part = lax.dynamic_slice_in_dim(queries, start, block, 0)
            masked, allowed = scores_of(queries_part, keys, start)
            top = lax.optimization_barrier(jnp.max(masked, axis=-1, keepdims=True))
            total = lax.optimization_barrier(jnp.sum(jnp.where(allowed, jnp.exp(masked - top), 0.0), axis=-1, keepdims=True))
            logsum = top + jnp.log(total)
            probs = jnp.where(allowed, jnp.exp(masked - logsum), 0.0).astype(jnp.bfloat16)
            outcome = jnp.einsum('hqk,khd->qhd', probs.astype(jnp.float32), values.astype(jnp.float32))
            return (outcome.astype(jnp.bfloat16), logsum[..., 0])
        attended, logsum = lax.map(forward_block, jnp.arange(blocks, dtype=jnp.int32))
        attended_rows = attended.reshape(LEN, D)
        hidden_one = rows_in + jnp.dot(attended_rows, dense_weight, preferred_element_type=jnp.float32) + bias_dense
        normed_two_low = norm_forward(hidden_one, gain_two, shift_two).astype(jnp.bfloat16)
        pre_act = jnp.dot(normed_two_low, up_weight, preferred_element_type=jnp.float32) + bias_up
        activated = gelu_tanh(pre_act).astype(jnp.bfloat16)
        output = (hidden_one + jnp.dot(activated, down_weight, preferred_element_type=jnp.float32) + bias_down).astype(jnp.bfloat16)
        cot_full = cotangent.astype(jnp.float32)
        grad_down_w = jnp.dot(activated.T, cotangent, preferred_element_type=jnp.float32)
        grad_down_b = lax.optimization_barrier(jnp.sum(cot_full, axis=0))
        grad_act = jnp.dot(cotangent, down_weight.T, preferred_element_type=jnp.float32)
        grad_pre = jax.vjp(gelu_tanh, pre_act)[1](grad_act)[0]
        grad_pre_low = grad_pre.astype(jnp.bfloat16)
        grad_up_w = jnp.dot(normed_two_low.T, grad_pre_low, preferred_element_type=jnp.float32)
        grad_up_b = lax.optimization_barrier(jnp.sum(grad_pre, axis=0)).reshape(FF // HD, HD)
        grad_normed_two = jnp.dot(grad_pre_low, up_weight.T, preferred_element_type=jnp.float32)
        back_two = jax.vjp(norm_forward, hidden_one, gain_two, shift_two)[1](grad_normed_two)
        grad_hidden = cot_full + back_two[0]
        grad_hidden_low = grad_hidden.astype(jnp.bfloat16)
        grad_dense_w = jnp.dot(attended_rows.T, grad_hidden_low, preferred_element_type=jnp.float32)
        grad_dense_b = lax.optimization_barrier(jnp.sum(grad_hidden, axis=0))
        grad_attended = jnp.dot(grad_hidden_low, dense_weight.T, preferred_element_type=jnp.float32).astype(jnp.bfloat16).reshape(LEN, H, HD)
        delta = lax.optimization_barrier(jnp.sum(grad_attended.astype(jnp.float32) * attended_rows.reshape(LEN, H, HD).astype(jnp.float32), axis=-1))

        def backward_block(carry, index):
            grad_keys, grad_values = carry
            start = index * block
            queries_part = lax.dynamic_slice_in_dim(queries, start, block, 0)
            out_grad = lax.dynamic_slice_in_dim(grad_attended, start, block, 0).astype(jnp.float32)
            delta_part = lax.dynamic_slice_in_dim(delta, start, block, 0).T
            masked, allowed = scores_of(queries_part, keys, start)
            probs = jnp.where(allowed, jnp.exp(masked - logsum[index][..., None]), 0.0)
            probs_low = probs.astype(jnp.bfloat16).astype(jnp.float32)
            grad_values = grad_values + jnp.einsum('hqk,qhd->khd', probs_low, out_grad)
            grad_probs = jnp.einsum('qhd,khd->hqk', out_grad, values.astype(jnp.float32))
            grad_scores = (probs * (grad_probs - delta_part[..., None]) * scale).astype(jnp.bfloat16).astype(jnp.float32)
            grad_query_part = jnp.einsum('hqk,khd->qhd', grad_scores, keys.astype(jnp.float32))
            grad_keys = grad_keys + jnp.einsum('hqk,qhd->khd', grad_scores, queries_part.astype(jnp.float32))
            return ((grad_keys, grad_values), grad_query_part)
        empty = jnp.zeros((LEN, H, HD), jnp.float32)
        (grad_keys, grad_values), grad_query = lax.scan(backward_block, (empty, empty), jnp.arange(blocks, dtype=jnp.int32))
        grad_query = grad_query.reshape(LEN, D)
        grad_keys = grad_keys.reshape(LEN, D)
        grad_values = grad_values.reshape(LEN, D)
        lows = (grad_query.astype(jnp.bfloat16), grad_keys.astype(jnp.bfloat16), grad_values.astype(jnp.bfloat16))
        grad_qkv_w = jnp.stack([jnp.dot(normed_low.T, member, preferred_element_type=jnp.float32) for member in lows])
        grad_qv_b = jnp.stack([lax.optimization_barrier(jnp.sum(grad_query, axis=0)), lax.optimization_barrier(jnp.sum(grad_values, axis=0))]).reshape(2, H, HD)
        grad_normed_one = jnp.dot(lows[0], qkv_weight[0].T, preferred_element_type=jnp.float32)
        grad_normed_one = grad_normed_one + jnp.dot(lows[1], qkv_weight[1].T, preferred_element_type=jnp.float32)
        grad_normed_one = grad_normed_one + jnp.dot(lows[2], qkv_weight[2].T, preferred_element_type=jnp.float32)
        back_one = jax.vjp(norm_forward, rows_in, gain_one, shift_one)[1](grad_normed_one)
        grad_in = grad_hidden + back_one[0]
        terms = (back_one[1], back_one[2], grad_qkv_w, grad_qv_b, grad_dense_w, grad_dense_b, back_two[1], back_two[2], grad_up_w, grad_up_b, grad_down_w, grad_down_b)
        grads = jax.tree.map(lambda first, second: first + second, grads, terms)
        return (grads, (output, grad_in))
    start_grads = (jnp.zeros((D,), jnp.float32), jnp.zeros((D,), jnp.float32), jnp.zeros((3, D, D), jnp.float32), jnp.zeros((2, H, HD), jnp.float32), jnp.zeros((D, D), jnp.float32), jnp.zeros((D,), jnp.float32), jnp.zeros((D,), jnp.float32), jnp.zeros((D,), jnp.float32), jnp.zeros((D, FF), jnp.float32), jnp.zeros((FF // HD, HD), jnp.float32), jnp.zeros((FF, D), jnp.float32), jnp.zeros((D,), jnp.float32))
    grads, (outputs, grad_inputs) = lax.scan(one_sequence, start_grads, (block_input, out_cotangent))
    return (outputs, grad_inputs, grads[0], grads[1], grads[2], grads[3], grads[4], grads[5], grads[6], grads[7], grads[8], grads[9], grads[10], grads[11])
```

```python
import math

import jax
import jax.numpy as jnp
import numpy as np
from jax import lax
from jax.experimental import pallas as pl
from jax.experimental.pallas import tpu as pltpu
from jax.sharding import PartitionSpec as P

H = 16
HD = 64
EPS = 1e-05
NEG = -1e30
F32 = jnp.float32
BF16 = jnp.bfloat16


DP, CTX, TEN, SEQ = 0, 1, 2, 3
GAIN1, SHIFT1, GAIN2, SHIFT2, DENSE_B, DOWN_B, QV_B, UP_B = range(8)


def nn(a, b):
    return lax.dot_general(a, b, (((1,), (0,)), ((), ())), preferred_element_type=F32)


def nt(a, b):
    return lax.dot_general(a, b, (((1,), (1,)), ((), ())), preferred_element_type=F32)


def tn(a, b):
    return lax.dot_general(a, b, (((0,), (0,)), ((), ())), preferred_element_type=F32)


def call(body, scalars, ins, outs, alias=None, name=None):
    def spec(arr, how):
        if how == "smem":
            return pl.BlockSpec(memory_space=pltpu.SMEM)
        if how == "any":
            return pl.BlockSpec(memory_space=pl.ANY)
        rank = len(arr.shape)
        if how == "seq":
            block = (pl.Squeezed(),) + tuple(arr.shape[1:])
            return pl.BlockSpec(block, lambda i, s: (s[SEQ],) + (0,) * (rank - 1))
        return pl.BlockSpec(tuple(arr.shape), lambda i, s: (0,) * rank)

    grid_spec = pltpu.PrefetchScalarGridSpec(
        num_scalar_prefetch=1,
        grid=(1,),
        in_specs=[spec(a, how) for a, how in ins],
        out_specs=[spec(o, how) for o, how in outs],
    )
    aliases = {} if alias is None else {1 + i: o for i, o in alias.items()}
    return pl.pallas_call(
        body,
        grid_spec=grid_spec,
        out_shape=[o for o, _ in outs],
        input_output_aliases=aliases,
        name=name,
        compiler_params=pltpu.CompilerParams(vmem_limit_bytes=56 * 1024 * 1024),
    )(scalars, *[a for a, _ in ins])


def shape(dims, kind):
    return jax.ShapeDtypeStruct(tuple(dims), kind)


def own_cols(sc, j, w):
    return pl.ds(pl.multiple_of(jnp.bitwise_xor(j, sc[DP]) * w, w), w)


def block(j, w):
    return slice(j * w, (j + 1) * w)


def moments(parts, dim):
    mean = sum(jnp.sum(p, axis=-1, keepdims=True) for p in parts) / dim
    centred = [p - mean for p in parts]
    var = sum(jnp.sum(c * c, axis=-1, keepdims=True) for c in centred) / dim
    scale = lax.rsqrt(var + EPS)
    return centred, scale


def norm_back(grads, hats, gains, scale, dim):
    scaled = [g * gain for g, gain in zip(grads, gains)]
    first = sum(jnp.sum(s, axis=-1, keepdims=True) for s in scaled) / dim
    second = sum(jnp.sum(s * h, axis=-1, keepdims=True) for s, h in zip(scaled, hats)) / dim
    return [scale * (s - first - h * second) for s, h in zip(scaled, hats)]


def rowsum(value):
    return jnp.sum(value, axis=0, keepdims=True)


def row_of(refs, row):
    return [ref[row : row + 1, :].astype(F32) for ref in refs]


def qkv_kernel(nb, nr, sc, *refs):
    xs = refs[:nr]
    weights = refs[nr : nr + nb]
    small = refs[nr + nb : nr + 2 * nb]
    q_ref, *rest = refs[nr + 2 * nb :]
    kvs, normed_ref = rest[: 2 * nr], rest[2 * nr]
    seqs, tokens, dim = xs[0].shape
    w = dim // nb
    cols = weights[0].shape[2]
    piece = HD // nb
    heads = cols // HD
    per = heads * piece
    row = lax.broadcasted_iota(jnp.int32, (2 * per, cols), 0)
    col = lax.broadcasted_iota(jnp.int32, (2 * per, cols), 1)
    bias = []
    for m in range(2):
        total = jnp.zeros((16, cols), F32)
        at = row - m * per
        ok = (at >= 0) & (at < per)
        for j in range(nb):
            goal = lax.div(at, piece) * HD + jnp.bitwise_xor(j, sc[DP]) * piece + lax.rem(at, piece)
            place = jnp.where(ok & (col == goal), 1.0, 0.0).astype(BF16)
            line = jnp.broadcast_to(small[j][QV_B : QV_B + 1, : 2 * per], (16, 2 * per))
            total = total + nn(line.astype(BF16), place)
        bias.append(total[0:1])
    gains = row_of(small, GAIN1)
    shifts = row_of(small, SHIFT1)
    for r in range(nr):
        parts = [
            xs[r][:, :, own_cols(sc, j, w)].reshape(seqs * tokens, w).astype(F32) for j in range(nb)
        ]
        centred, scale = moments(parts, dim)
        normed = [
            (c * scale * g + s).astype(BF16) for c, g, s in zip(centred, gains, shifts)
        ]
        if r == 0:
            for j in range(nb):
                normed_ref[:, block(j, w)] = normed[j]
            q = sum(nn(normed[j], weights[j][0]) for j in range(nb)) + bias[0]
            q_ref[...] = q.astype(BF16).reshape(seqs, tokens, cols)
        k = sum(nn(normed[j], weights[j][1]) for j in range(nb))
        v = sum(nn(normed[j], weights[j][2]) for j in range(nb)) + bias[1]
        kvs[2 * r][...] = k.astype(BF16).reshape(seqs, tokens, cols)
        kvs[2 * r + 1][...] = v.astype(BF16).reshape(seqs, tokens, cols)


def probs_of(sc, slope, q, keys, nr):
    tokens = q.shape[0]
    row = lax.broadcasted_iota(jnp.int32, (tokens, tokens), 0)
    col = lax.broadcasted_iota(jnp.int32, (tokens, tokens), 1)
    scores = []
    for r in range(nr):
        distance = row - col + r * tokens
        allowed = (distance >= 0) & (sc[CTX] >= r)
        raw = nt(q, keys[r]) * (HD**-0.5) - slope * distance.astype(F32)
        scores.append((jnp.where(allowed, raw, NEG), allowed))
    top = scores[0][0].max(axis=-1, keepdims=True)
    for masked, _ in scores[1:]:
        top = jnp.maximum(top, masked.max(axis=-1, keepdims=True))
    powers = [jnp.where(ok, jnp.exp(masked - top), 0.0) for masked, ok in scores]
    total = sum(jnp.sum(p, axis=-1, keepdims=True) for p in powers)
    inverse = 1.0 / total
    return [p * inverse for p in powers]


def attend_kernel(nb, nr, sc, slopes, q_ref, *refs):
    keys, values = refs[: 2 * nr : 2], refs[1 : 2 * nr : 2]
    dense = refs[2 * nr : 2 * nr + nb]
    att_ref, part_ref = refs[2 * nr + nb], refs[2 * nr + nb + 1]
    tokens, cols = q_ref.shape
    w = dense[0].shape[1]
    heads = cols // HD
    pieces = []
    for h in range(heads):
        at = slice(h * HD, (h + 1) * HD)
        slope = slopes[sc[TEN] * heads + h]
        probs = probs_of(sc, slope, q_ref[:, at], [k[:, at] for k in keys], nr)
        pieces.append(sum(nn(p.astype(BF16), v[:, at]) for p, v in zip(probs, values)))
    attended = jnp.concatenate(pieces, axis=1).astype(BF16)
    att_ref[...] = attended
    for j in range(nb):
        part_ref[:, block(j, w)] = nn(attended, dense[j][...]).astype(BF16)


def act_grad_kernel(nb, sc, cot_ref, *refs):
    down = refs[:nb]
    ga_ref, sum_ref = refs[nb:]
    rows, dim = cot_ref.shape
    w = dim // nb
    total = None
    for j in range(nb):
        cot = cot_ref[:, own_cols(sc, j, w)]
        term = nt(cot, down[j][...])
        total = term if total is None else total + term
        sum_ref[:, block(j, w)] = rowsum(cot.astype(F32))
    ga_ref[...] = total


def hidden_of(nb, sc, x_ref, total_ref, small, w):
    bias = row_of(small, DENSE_B)
    return [
        x_ref[:, own_cols(sc, j, w)].astype(F32) + total_ref[:, block(j, w)].astype(F32) + bias[j]
        for j in range(nb)
    ]


def mlp_kernel(nb, n_alias, sc, total_ref, x_ref, ga_ref, upb_ref, *refs):
    up = refs[:nb]
    small = refs[nb : 2 * nb]
    n2_ref, act_ref, low_ref, gpb_ref, part_ref = refs[2 * nb + n_alias :]
    tokens, dim = x_ref.shape
    w = dim // nb
    hidden = hidden_of(nb, sc, x_ref, total_ref, small, w)
    centred, scale = moments(hidden, dim)
    gains, shifts = row_of(small, GAIN2), row_of(small, SHIFT2)
    pre = upb_ref[...]
    for j in range(nb):
        normed = (centred[j] * scale * gains[j] + shifts[j]).astype(BF16)
        n2_ref[:, block(j, w)] = normed
        pre = pre + nn(normed, up[j][...])
    c = math.sqrt(2.0 / math.pi)
    square = pre * pre
    t = jnp.tanh(c * (pre + 0.044715 * (square * pre)))
    half = 0.5 * (1.0 + t)
    act_ref[...] = (pre * half).astype(BF16)
    slope = half + 0.5 * pre * (1.0 - t * t) * (c * (1.0 + 3.0 * 0.044715 * square))
    grad = slope * ga_ref[...]
    gpb_ref[...] = rowsum(grad)
    low = grad.astype(BF16)
    low_ref[...] = low
    for j in range(nb):
        part_ref[:, block(j, w)] = nt(low, up[j][...]).astype(BF16)


def down_kernel(nb, sc, act_ref, *refs):
    down, part_ref = refs[:nb], refs[nb]
    w = down[0].shape[1]
    for j in range(nb):
        part_ref[:, block(j, w)] = nn(act_ref[...], down[j][...]).astype(BF16)


def output_kernel(nb, n_alias, sc, total1_ref, total4_ref, x_ref, *refs):
    small = refs[:nb]
    out_ref = refs[nb + n_alias]
    w = small[0].shape[1]
    bias = row_of(small, DOWN_B)
    hidden = hidden_of(nb, sc, x_ref, total1_ref, small, w)
    for j in range(nb):
        value = hidden[j] + total4_ref[:, block(j, w)].astype(F32) + bias[j]
        out_ref[:, own_cols(sc, j, w)] = value.astype(BF16)


def back_kernel(nb, nr, n_alias, sc, slopes, total2_ref, total1_ref, x_ref, cot_ref, att_ref, q_ref, *refs):
    keys, values = refs[: 2 * nr : 2], refs[1 : 2 * nr : 2]
    refs = refs[2 * nr :]
    dense, small = refs[:nb], refs[nb : 2 * nb]
    gh_ref, ghl_ref, vec_ref, dq_ref, qvb_ref, *dkv = refs[2 * nb + n_alias :]
    tokens, dim = x_ref.shape
    cols = q_ref.shape[1]
    heads = cols // HD
    w = dim // nb
    hidden = hidden_of(nb, sc, x_ref, total1_ref, small, w)
    centred, scale = moments(hidden, dim)
    hats = [c * scale for c in centred]
    grads = [total2_ref[:, block(j, w)].astype(F32) for j in range(nb)]
    back = norm_back(grads, hats, row_of(small, GAIN2), scale, dim)
    ga = None
    for j in range(nb):
        gh = cot_ref[:, own_cols(sc, j, w)].astype(F32) + back[j]
        gh_ref[:, block(j, w)] = gh
        vec_ref[0:1, block(j, w)] = rowsum(grads[j] * hats[j])
        vec_ref[1:2, block(j, w)] = rowsum(grads[j])
        vec_ref[2:3, block(j, w)] = rowsum(gh)
        low = gh.astype(BF16)
        ghl_ref[:, block(j, w)] = low
        term = nt(low, dense[j][...])
        ga = term if ga is None else ga + term
    ga = ga.astype(BF16)
    prod = ga.astype(F32) * att_ref[...].astype(F32)
    dqs, dks, dvs = [], [[] for _ in range(nr)], [[] for _ in range(nr)]
    for h in range(heads):
        at = slice(h * HD, (h + 1) * HD)
        slope = slopes[sc[TEN] * heads + h]
        q, go = q_ref[:, at], ga[:, at]
        probs = probs_of(sc, slope, q, [k[:, at] for k in keys], nr)
        delta = jnp.sum(prod[:, at], axis=-1, keepdims=True)
        dq = None
        for r in range(nr):
            dp = nt(go, values[r][:, at])
            ds = (probs[r] * (dp - delta) * (HD**-0.5)).astype(BF16)
            term = nn(ds, keys[r][:, at])
            dq = term if dq is None else dq + term
            dks[r].append(tn(ds, q))
            dvs[r].append(tn(probs[r].astype(BF16), go))
        dqs.append(dq)
    dq = jnp.concatenate(dqs, axis=1)
    dq_ref[...] = dq.astype(BF16)
    vsum = None
    for r in range(nr):
        dk = jnp.concatenate(dks[r], axis=1)
        dv = jnp.concatenate(dvs[r], axis=1)
        dkv[r][:, :cols] = dk.astype(dkv[r].dtype)
        dkv[r][:, cols:] = dv.astype(dkv[r].dtype)
        term = rowsum(dv)
        vsum = term if vsum is None else vsum + term
    qvb_ref[0:1, :] = rowsum(dq)
    qvb_ref[1:2, :] = vsum


def inner_kernel(nb, nr, n_alias, sc, dq_ref, x_ref, *refs):
    dkv = refs[:nr]
    weights = refs[nr : nr + nb]
    low_ref, vec_ref, part_ref = refs[nr + nb + n_alias :]
    tokens, dim = x_ref.shape
    w = dim // nb
    cols = dq_ref.shape[1]
    total = dkv[0][...]
    for r in range(1, nr):
        total = total + dkv[r][...].astype(F32)
    total = total.astype(BF16)
    lows = [dq_ref[...], total[:, :cols], total[:, cols:]]
    for m in range(3):
        low_ref[:, m * cols : (m + 1) * cols] = lows[m]
    parts = [x_ref[:, own_cols(sc, j, w)].astype(F32) for j in range(nb)]
    centred, scale = moments(parts, dim)
    for j in range(nb):
        part = sum(nt(lows[m], weights[j][m]) for m in range(3))
        part_ref[:, block(j, w)] = part.astype(BF16)
        vec_ref[0:1, block(j, w)] = rowsum(part * (centred[j] * scale))
        vec_ref[1:2, block(j, w)] = rowsum(part)


def last_kernel(nb, n_alias, sc, total_ref, x_ref, gh_ref, *refs):
    small = refs[:nb]
    out_ref = refs[nb + n_alias]
    tokens, dim = x_ref.shape
    w = dim // nb
    parts = [x_ref[:, own_cols(sc, j, w)].astype(F32) for j in range(nb)]
    centred, scale = moments(parts, dim)
    hats = [c * scale for c in centred]
    grads = [total_ref[:, block(j, w)].astype(F32) for j in range(nb)]
    back = norm_back(grads, hats, row_of(small, GAIN1), scale, dim)
    for j in range(nb):
        out_ref[:, own_cols(sc, j, w)] = gh_ref[:, block(j, w)] + back[j]


def down_weight_kernel(nb, sc, act_ref, cot_ref, keep_ref, send_ref):
    w = keep_ref.shape[2]
    left = act_ref[...].T
    for j in range(nb):
        out = nn(left, cot_ref[:, own_cols(sc, j, w)]).astype(BF16)
        (send_ref if j & 1 else keep_ref)[j >> 1] = out


def up_weight_kernel(nb, sc, n2_ref, low_ref, keep_ref, send_ref):
    w = keep_ref.shape[1]
    left = n2_ref[...].T
    for j in range(nb):
        out = nn(left[block(j, w)], low_ref[...]).astype(BF16)
        (send_ref if j & 1 else keep_ref)[j >> 1] = out


def qkv_weight_kernel(nb, sc, normed_ref, low_ref, att_ref, ghl_ref, keep_ref, send_ref):
    dim = normed_ref.shape[1]
    w = dim // nb
    cols = att_ref.shape[1]
    left = normed_ref[...].T
    att = att_ref[...].T
    for j in range(nb):
        goal = send_ref if j & 1 else keep_ref
        out = nn(left[block(j, w)], low_ref[...]).astype(BF16)
        for m in range(3):
            goal[j >> 1, m] = out[:, m * cols : (m + 1) * cols]
        goal[j >> 1, 3] = nn(att, ghl_ref[:, block(j, w)]).astype(BF16)


def exchange(value, axis, bit):
    n = lax.axis_size(axis)
    return lax.ppermute(value, axis, [(i, i ^ bit) for i in range(n)])


def gather_relative(own, after=None):
    n = lax.axis_size("dp")
    if after is not None:
        own, _ = lax.optimization_barrier((own, after))
    held = {0: own}
    bit = n // 2
    while bit:
        for j in list(held):
            held[j | bit] = exchange(held[j], "dp", bit)
        bit //= 2
    return [held[j] for j in range(n)]


def add(a, b):
    return (a.astype(F32) + b.astype(F32)).astype(a.dtype)


def tensor_sum(first, second):
    n = lax.axis_size("tensor")
    kept = add(second, exchange(first, "tensor", 1))
    bit = 2
    while bit < n:
        kept = add(kept, exchange(kept, "tensor", bit))
        bit *= 2
    return kept, exchange(kept, "tensor", 1)


def owner_sum(keep, send):
    n = lax.axis_size("dp")
    total = add(keep, exchange(send, "dp", 1))
    bit = n // 2
    while bit > 1:
        half = total.shape[0] // 2
        total = add(total[:half], exchange(total[half:], "dp", bit))
        bit //= 2
    total = total[0]
    bit = 1
    while bit < lax.axis_size("ctx"):
        other = exchange(total, "ctx", bit)
        bit *= 2
        total = add(total, other) if bit < lax.axis_size("ctx") else total.astype(F32) + other.astype(F32)
    return total.astype(F32)


def on_device(
    block_input,
    out_cotangent,
    gain_attn,
    shift_attn,
    qkv_weight,
    qv_bias,
    dense_weight,
    dense_bias,
    gain_mlp,
    shift_mlp,
    up_weight,
    up_bias,
    down_weight,
    down_bias,
):
    nb = lax.axis_size("dp")
    nr = lax.axis_size("ctx")
    nt_dev = lax.axis_size("tensor")
    seqs, tokens, dim = block_input.shape
    rows = seqs * tokens
    w = dim // nb
    cols = qkv_weight.shape[2]
    ff = up_weight.shape[1]
    dp = lax.axis_index("dp")
    me = lax.axis_index("tensor") & 1
    place = [dp, lax.axis_index("ctx"), lax.axis_index("tensor")]
    sc = [jnp.stack(place + [s]).astype(jnp.int32) for s in (me, 1 - me)]
    slopes = jnp.asarray(2.0 ** (-8.0 * (np.arange(H) + 1.0) / H), F32)

    qkv = gather_relative(qkv_weight)
    pad = jnp.zeros((w - qv_bias.size,), BF16)
    small_own = jnp.stack(
        [
            gain_attn,
            shift_attn,
            gain_mlp,
            shift_mlp,
            dense_bias,
            down_bias,
            jnp.concatenate([qv_bias.reshape(-1), pad]),
            up_bias.reshape(-1),
        ]
    )
    small = gather_relative(small_own)
    x_blocks = [block_input]
    for r in range(1, nr):
        x_blocks.append(
            lax.ppermute(block_input, "ctx", [(i, i + r) for i in range(nr - r)])
        )
    dense = gather_relative(dense_weight, qkv[nb // 2])
    up = gather_relative(up_weight, dense[nb // 2])
    down = gather_relative(down_weight, up[nb // 2])

    order = jnp.arange(nb, dtype=jnp.int32) ^ dp
    per = up_bias.shape[1]
    upb = jnp.stack([s[UP_B].reshape(-1, per) for s in small])
    upb = jnp.take(upb, order, axis=0).transpose(1, 0, 2).reshape(1, ff).astype(F32)

    head_shape = shape((seqs, tokens, cols), BF16)
    q, *rest = call(
        lambda *a: qkv_kernel(nb, nr, *a),
        sc[0],
        [(x, "all") for x in x_blocks] + [(a, "all") for a in qkv] + [(a, "all") for a in small],
        [(head_shape, "all")] * (1 + 2 * nr) + [(shape((rows, dim), BF16), "all")],
        name="qkv",
    )
    kvs, normed = rest[: 2 * nr], rest[2 * nr]

    tok_d = shape((tokens, dim), BF16)
    tok_c = shape((tokens, cols), BF16)

    def attend(s):
        return call(
            lambda *a: attend_kernel(nb, nr, *a),
            s,
            [(slopes, "smem"), (q, "seq")]
            + [(a, "seq") for a in kvs]
            + [(a, "all") for a in dense],
            [(tok_c, "all"), (tok_d, "all")],
            name="attend",
        )

    att_b, part_b = attend(sc[1])
    att_a, part_a = attend(sc[0])
    total1_a, total1_b = tensor_sum(part_b, part_a)

    cot_rows = out_cotangent.reshape(rows, dim)
    grad_act, cot_sum = call(
        lambda *a: act_grad_kernel(nb, *a),
        sc[0],
        [(cot_rows, "all")] + [(a, "all") for a in down],
        [(shape((rows, ff), F32), "all"), (shape((1, dim), F32), "all")],
        name="act_grad",
    )
    grad_act = grad_act.reshape(seqs, tokens, ff)

    full_d = shape((seqs, tokens, dim), BF16)
    full_f = shape((seqs, tokens, ff), BF16)

    def mlp(s, total, before):
        return call(
            lambda *a: mlp_kernel(nb, len(before), *a),
            s,
            [(total, "all"), (block_input, "seq"), (grad_act, "seq"), (upb, "all")]
            + [(a, "all") for a in up]
            + [(a, "all") for a in small]
            + [(a, "any") for a in before],
            [(full_d, "seq"), (full_f, "seq"), (full_f, "seq")]
            + [(shape((1, ff), F32), "all"), (tok_d, "all")],
            alias={4 + 2 * nb + i: i for i in range(len(before))},
            name="mlp",
        )

    n2, act, low, gpb_a, part_a = mlp(sc[0], total1_a, ())
    n2, act, low, gpb_b, part_b = mlp(sc[1], total1_b, (n2, act, low))
    total2_b, total2_a = tensor_sum(part_a, part_b)

    def down_part(s):
        return call(
            lambda *a: down_kernel(nb, *a),
            s,
            [(act, "seq")] + [(a, "all") for a in down],
            [(tok_d, "all")],
            name="down",
        )[0]

    down_a, down_b = down_part(sc[0]), down_part(sc[1])
    total4_b, total4_a = tensor_sum(down_a, down_b)

    def output(s, total1, total4, before):
        return call(
            lambda *a: output_kernel(nb, len(before), *a),
            s,
            [(total1, "all"), (total4, "all"), (block_input, "seq")]
            + [(a, "all") for a in small]
            + [(a, "any") for a in before],
            [(full_d, "seq")],
            alias={3 + nb + i: i for i in range(len(before))},
            name="output",
        )

    out = output(sc[1], total1_b, total4_b, ())
    out = output(sc[0], total1_a, total4_a, tuple(out))[0]

    act_rows, n2_rows, low_rows = (
        act.reshape(rows, ff),
        n2.reshape(rows, dim),
        low.reshape(rows, ff),
    )
    pair = nb // 2
    down_keep, down_send = call(
        lambda *a: down_weight_kernel(nb, *a),
        sc[0],
        [(act_rows, "all"), (cot_rows, "all")],
        [(shape((pair, ff, w), BF16), "all")] * 2,
        name="down_weight",
    )
    up_keep, up_send = call(
        lambda *a: up_weight_kernel(nb, *a),
        sc[0],
        [(n2_rows, "all"), (low_rows, "all")],
        [(shape((pair, w, ff), BF16), "all")] * 2,
        name="up_weight",
    )
    grad_down = owner_sum(down_keep, down_send)
    grad_up = owner_sum(up_keep, up_send)

    full_32 = shape((seqs, tokens, dim), F32)

    def back(s, total2, total1, att, before):
        return call(
            lambda *a: back_kernel(nb, nr, len(before), *a),
            s,
            [(slopes, "smem"), (total2, "all"), (total1, "all"), (block_input, "seq")]
            + [(out_cotangent, "seq"), (att, "all"), (q, "seq")]
            + [(a, "seq") for a in kvs]
            + [(a, "all") for a in dense]
            + [(a, "all") for a in small]
            + [(a, "any") for a in before],
            [(full_32, "seq"), (full_d, "seq"), (shape((3, dim), F32), "all"), (tok_c, "all")]
            + [(shape((2, cols), F32), "all"), (shape((tokens, 2 * cols), F32), "all")]
            + [(shape((tokens, 2 * cols), BF16), "all")] * (nr - 1),
            alias={7 + 2 * nr + 2 * nb + i: i for i in range(len(before))},
            name="back",
        )

    gh, ghl, vec_b, dq_b, qvb_b, *dkv_b = back(sc[1], total2_b, total1_b, att_b, ())
    gh, ghl, vec_a, dq_a, qvb_a, *dkv_a = back(sc[0], total2_a, total1_a, att_a, (gh, ghl))

    def home(dkv):
        return [dkv[0]] + [
            lax.ppermute(dkv[r], "ctx", [(i + r, i) for i in range(nr - r)]) for r in range(1, nr)
        ]

    dkv_b, dkv_a = home(dkv_b), home(dkv_a)
    full_3c = shape((seqs, tokens, 3 * cols), BF16)

    def inner(s, dq, dkv, before):
        return call(
            lambda *a: inner_kernel(nb, nr, len(before), *a),
            s,
            [(dq, "all"), (block_input, "seq")]
            + [(a, "all") for a in dkv]
            + [(a, "all") for a in qkv]
            + [(a, "any") for a in before],
            [(full_3c, "seq"), (shape((2, dim), F32), "all"), (tok_d, "all")],
            alias={2 + nr + nb + i: i for i in range(len(before))},
            name="inner",
        )

    lows, vec1_b, part_b = inner(sc[1], dq_b, dkv_b, ())
    lows, vec1_a, part_a = inner(sc[0], dq_a, dkv_a, (lows,))
    total3_a, total3_b = tensor_sum(part_b, part_a)

    qkv_keep, qkv_send = call(
        lambda *a: qkv_weight_kernel(nb, *a),
        sc[0],
        [(normed, "all"), (lows.reshape(rows, 3 * cols), "all")]
        + [(jnp.where(me == 0, jnp.stack([att_a, att_b]), jnp.stack([att_b, att_a])).reshape(rows, cols), "all")]
        + [(ghl.reshape(rows, dim), "all")],
        [(shape((pair, 4, w, cols), BF16), "all")] * 2,
        name="qkv_weight",
    )
    grad_heads = owner_sum(qkv_keep, qkv_send)

    vec1 = vec1_a + vec1_b
    bit = 1
    while bit < nt_dev:
        vec1 = vec1 + exchange(vec1, "tensor", bit)
        bit *= 2
    vec2 = vec_a + vec_b
    by_block = jnp.concatenate([vec1, vec2, cot_sum]).reshape(6, nb, w).transpose(1, 0, 2)
    qvb = (qvb_a + qvb_b).reshape(2, cols // HD, nb, HD // nb).transpose(2, 0, 1, 3)
    qvb = jnp.take(qvb.reshape(nb, 1, -1), order, axis=0)
    qvb = jnp.pad(qvb, ((0, 0), (0, 0), (0, w - qvb.shape[2])))
    gpb = (gpb_a + gpb_b).reshape(-1, nb, per).transpose(1, 0, 2)
    gpb = jnp.take(gpb.reshape(nb, 1, -1), order, axis=0)
    vectors = jnp.concatenate([by_block, qvb, gpb], axis=1)
    vectors = owner_sum(vectors[0::2], vectors[1::2])

    def last(s, total3, before):
        return call(
            lambda *a: last_kernel(nb, len(before), *a),
            s,
            [(total3, "all"), (block_input, "seq"), (gh, "seq")]
            + [(a, "all") for a in small]
            + [(a, "any") for a in before],
            [(full_32, "seq")],
            alias={3 + nb + i: i for i in range(len(before))},
            name="last",
        )

    grad_in = last(sc[0], total3_a, ())
    grad_in = last(sc[1], total3_b, tuple(grad_in))[0]

    return (
        out,
        grad_in,
        vectors[0],
        vectors[1],
        grad_heads[:3],
        vectors[6, : qv_bias.size].reshape(qv_bias.shape),
        grad_heads[3],
        vectors[4],
        vectors[2],
        vectors[3],
        grad_up,
        vectors[7].reshape(up_bias.shape),
        grad_down,
        vectors[5],
    )


def solution(mesh):
    placed = (
        P("dp", "ctx", None),
        P("dp", "ctx", None),
        P("dp"),
        P("dp"),
        P(None, "dp", "tensor"),
        P(None, "tensor", "dp"),
        P("tensor", "dp"),
        P("dp"),
        P("dp"),
        P("dp"),
        P("dp", "tensor"),
        P("tensor", "dp"),
        P("tensor", "dp"),
        P("dp"),
    )
    return jax.shard_map(
        on_device,
        mesh=mesh,
        in_specs=placed,
        out_specs=(
            P("dp", "ctx", None),
            P("dp", "ctx", None),
            P("dp"),
            P("dp"),
            P(None, "dp", "tensor"),
            P(None, "tensor", "dp"),
            P("tensor", "dp"),
            P("dp"),
            P("dp"),
            P("dp"),
            P("dp", "tensor"),
            P("tensor", "dp"),
            P("tensor", "dp"),
            P("dp"),
        ),
        check_vma=False,
    )
```
